32 devices in a mesh: grp: 2 (over x), tile: 16 (over z, y, core).
Axes of the slice: x: 2, y: 2, z: 4, core: 2. Of those that a mesh axis runs over, the one named last changes fastest.
Arguments:
- x_tiles: bfloat16 [32, 16, 16, 256], P(('grp', 'tile')), parts along dimension 0, may hold values from -6 to 6
- h_tiles: bfloat16 [32, 16, 16, 256], P(('grp', 'tile')), parts along dimension 0, may hold values from -6 to 6
- grad_out: bfloat16 [32, 16, 16, 256], P(('grp', 'tile')), parts along dimension 0, may hold values from -6 to 6
- w_gate: bfloat16 [4608, 512], replicated, may hold values from -0.09375 to 0.09375
- b_gate: float32 [512], replicated, may hold values from -3 to 3
- w_cand: bfloat16 [4608, 256], replicated, may hold values from -0.09375 to 0.09375
- b_cand: float32 [256], replicated, may hold values from -3 to 3
- partner_edge: int32 [16, 4], replicated, may hold values from 0 to 63, as said below
- edge_flip: int32 [16, 4], replicated, may hold values from 0 to 1, as said below
- tile_slot: int32 [16], replicated, may hold values from 0 to 15, as said below
Outputs:
- grad_x: bfloat16 [32, 16, 16, 256], P(('grp', 'tile')), parts along dimension 0
- grad_h: bfloat16 [32, 16, 16, 256], P(('grp', 'tile')), parts along dimension 0
- grad_w_gate: float32 [9216, 512], P(('grp', 'tile')), parts along dimension 0
- grad_w_cand: float32 [9216, 256], P(('grp', 'tile')), parts along dimension 0
The draws below stay inside these ranges and needn't reach their ends.
There are 2 independent parts, one for each index of `grp`. The reference program is written for one: setup_inputs(seed, part) draws one part's arguments, and reference() takes and returns one part's arrays. A program takes and returns all parts, laid end to end along the dimension named above; an argument that names none is the same for every part. Nothing has to cross between parts.
Inputs may be any that keep to these rules, and one draw needn't show every extreme that they name: `partner_edge`: the matching is an involution over all 64 tile edges and never joins a tile to itself; of each tile's four edges, two meet edges of the tile in the next slot and two meet edges of the tile in the previous slot, slots counted cyclically. `edge_flip`: equal at both edges of a matched pair. `tile_slot`: A permutation of the slots.
All inputs are finite; a program needn't handle non-finite values.
Results may differ from the reference program's by a relative error of at most 0.0051.
Values may be sent and summed in bfloat16 or wider, within the bound.
A program may use at most 128 MiB of HBM per device.

```python
import jax
import jax.numpy as jnp

C = 256
S = 16
TILES = 16


def matching(base_key):
    tile_count = TILES
    key_order, key_flip, key_slot = jax.random.split(jax.random.fold_in(base_key, 7), 3)
    orders = jax.vmap(lambda sub_key: jax.random.permutation(sub_key, 4))(jax.random.split(key_order, tile_count)).astype(jnp.int32)
    slot_ids = jnp.arange(tile_count, dtype=jnp.int32)
    next_slot = (slot_ids + 1) % tile_count
    right_ends = (slot_ids[:, None] * 4 + orders[:, :2]).reshape(-1)
    left_ends = (next_slot[:, None] * 4 + orders[next_slot][:, 2:]).reshape(-1)
    partner_of = jnp.zeros((4 * tile_count,), jnp.int32).at[right_ends].set(left_ends).at[left_ends].set(right_ends)
    flip_draw = jax.random.randint(key_flip, (2 * tile_count,), 0, 2, dtype=jnp.int32)
    flip_table = jnp.zeros((4 * tile_count,), jnp.int32).at[right_ends].set(flip_draw).at[left_ends].set(flip_draw)
    tile_slot = jax.random.permutation(key_slot, tile_count).astype(jnp.int32)
    holder = jnp.zeros((tile_count,), jnp.int32).at[tile_slot].set(slot_ids)
    edge_ids = tile_slot[:, None] * 4 + jnp.arange(4, dtype=jnp.int32)[None, :]
    partners = partner_of[edge_ids]
    partner_tile = holder[partners // 4] * 4 + partners % 4
    return (partner_tile.astype(jnp.int32), flip_table[edge_ids], tile_slot)


def draw_partner_edge(key, part):
    return matching(key)[0]


def draw_edge_flip(key, part):
    return matching(key)[1]


def draw_tile_slot(key, part):
    return matching(key)[2]


def steps_of(own_key, extent, cuts, least, top_value):
    def one(axis_at, blocks):
        draws = jax.random.uniform(jax.random.fold_in(jax.random.fold_in(own_key, 6), axis_at), (blocks,), jnp.float32, least / len(cuts), top_value / len(cuts))
        return jnp.repeat(jnp.exp(draws), extent[axis_at] // blocks).reshape((-1,) + (1,) * (len(extent) - axis_at - 1))

    factor_of = one(*cuts[0])
    for cut in cuts[1:]:
        factor_of = factor_of * one(*cut)
    return factor_of


def centred(stream_key, dims, spread, bound, shards=(), kind=jnp.bfloat16):
    values = jax.random.normal(stream_key, dims, jnp.float32) * spread
    if len(shards) > 0:
        values = steps_of(stream_key, dims, shards, -0.22, 0.18) * values
    return jnp.clip(values, min=-bound, max=bound).astype(kind)


def setup_inputs(seed: int = 0, part: int = 0) -> dict:
    arg_keys = jax.random.split(jax.random.key(seed), 11)
    own_keys = jax.random.split(jax.random.fold_in(arg_keys[10], part), 11)
    x_tiles = centred(own_keys[0], (TILES, S, S, C), 1.0, 6.0, ((0, 16),))
    h_tiles = centred(own_keys[1], (TILES, S, S, C), 1.0, 6.0, ((0, 16),))
    grad_out = centred(own_keys[2], (TILES, S, S, C), 1.0, 6.0, ((0, 16),))
    w_gate = centred(arg_keys[3], (18 * C, 2 * C), (18 * C) ** -0.5, 0.09375)
    b_gate = centred(arg_keys[4], (2 * C,), 1.0, 3.0, (), jnp.float32)
    w_cand = centred(arg_keys[5], (18 * C, C), (18 * C) ** -0.5, 0.09375)
    b_cand = centred(arg_keys[6], (C,), 1.0, 3.0, (), jnp.float32)
    partner_edge = draw_partner_edge(jax.random.fold_in(arg_keys[10], 71), part)
    edge_flip = draw_edge_flip(jax.random.fold_in(arg_keys[10], 71), part)
    tile_slot = draw_tile_slot(jax.random.fold_in(arg_keys[10], 71), part)
    return dict(x_tiles=x_tiles, h_tiles=h_tiles, grad_out=grad_out, w_gate=w_gate, b_gate=b_gate, w_cand=w_cand, b_cand=b_cand, partner_edge=partner_edge, edge_flip=edge_flip, tile_slot=tile_slot)


def edge_strips(stack):
    return jnp.stack([stack[:, 0], stack[:, :, -1], stack[:, -1], stack[:, :, 0]], axis=1)


def routing(partner_edge, edge_flip, tile_slot):
    tile_count = tile_slot.shape[0]
    holder = jnp.zeros((tile_count,), jnp.int32).at[tile_slot].set(jnp.arange(tile_count, dtype=jnp.int32))
    partners = partner_edge[holder]
    target = tile_slot[partners // 4] * 4 + partners % 4
    return target.astype(jnp.int32), edge_flip[holder]


def deliver(strip_all, target, flipped):
    flat_strips = strip_all.reshape((-1,) + strip_all.shape[2:])
    picked = flat_strips[target.reshape(-1)].reshape(strip_all.shape)
    return jnp.where(flipped[:, :, None, None] == 1, picked[:, :, ::-1], picked)


def framed(stack, arrived):
    padded = jnp.pad(stack, ((0, 0), (1, 1), (1, 1), (0, 0)))
    padded = padded.at[:, 0, 1:-1].set(arrived[:, 0])
    padded = padded.at[:, 1:-1, -1].set(arrived[:, 1])
    padded = padded.at[:, -1, 1:-1].set(arrived[:, 2])
    padded = padded.at[:, 1:-1, 0].set(arrived[:, 3])
    return padded


def patches_of(padded):
    tile_side = padded.shape[1] - 2
    columns = [padded[:, row_tap:row_tap + tile_side, col_tap:col_tap + tile_side] for row_tap in range(3) for col_tap in range(3)]
    return jnp.concatenate(columns, axis=-1).reshape(-1, 9 * padded.shape[-1])


def unpatch(dpatch, tile_count, tile_side, channels):
    dpatch = dpatch.reshape(tile_count, tile_side, tile_side, 9, channels)
    result = jnp.zeros((tile_count, tile_side + 2, tile_side + 2, channels), jnp.float32)
    for row_tap in range(3):
        for col_tap in range(3):
            result = result.at[:, row_tap:row_tap + tile_side, col_tap:col_tap + tile_side].add(dpatch[:, :, :, row_tap * 3 + col_tap])
    return result


def rim_of(padded):
    return jnp.stack([padded[:, 0, 1:-1], padded[:, 1:-1, -1], padded[:, -1, 1:-1], padded[:, 1:-1, 0]], axis=1)


def settle(padded, arrived):
    interior = padded[:, 1:-1, 1:-1]
    interior = interior.at[:, 0].add(arrived[:, 0])
    interior = interior.at[:, :, -1].add(arrived[:, 1])
    interior = interior.at[:, -1].add(arrived[:, 2])
    interior = interior.at[:, :, 0].add(arrived[:, 3])
    return interior


def reference(x_tiles, h_tiles, grad_out, w_gate, b_gate, w_cand, b_cand, partner_edge, edge_flip, tile_slot):
    tile_count = x_tiles.shape[0]
    tile_side = x_tiles.shape[1]
    channels = x_tiles.shape[3]
    target, flipped = routing(partner_edge, edge_flip, tile_slot)
    joined = jnp.concatenate([x_tiles, h_tiles], axis=-1)
    patch_gate = patches_of(framed(joined, deliver(edge_strips(joined), target, flipped)))
    gate_act = jax.nn.sigmoid(jnp.dot(patch_gate, w_gate, preferred_element_type=jnp.float32) + b_gate)
    update_gate = gate_act[:, :channels]
    reset_gate = gate_act[:, channels:]
    h_flat = h_tiles.reshape(-1, channels).astype(jnp.float32)
    reset_h = (reset_gate * h_flat).astype(jnp.bfloat16)
    mixed = jnp.concatenate([x_tiles, reset_h.reshape(tile_count, tile_side, tile_side, channels)], axis=-1)
    patch_cand = patches_of(framed(mixed, deliver(edge_strips(mixed), target, flipped)))
    candidate = jnp.tanh(jnp.dot(patch_cand, w_cand, preferred_element_type=jnp.float32) + b_cand)
    grad_flat = grad_out.reshape(-1, channels).astype(jnp.float32)
    d_update = grad_flat * (candidate - h_flat)
    d_cand_pre = (grad_flat * update_gate * (1.0 - candidate * candidate)).astype(jnp.bfloat16)
    grad_w_cand = jnp.dot(patch_cand.T, d_cand_pre, preferred_element_type=jnp.float32)
    grid_cand = unpatch(jnp.dot(d_cand_pre, w_cand.T, preferred_element_type=jnp.float32), tile_count, tile_side, 2 * channels)
    back_cand = settle(grid_cand, deliver(rim_of(grid_cand), target, flipped))
    d_rh = back_cand[..., channels:].reshape(-1, channels)
    d_gate_pre = jnp.concatenate([d_update * update_gate * (1.0 - update_gate), d_rh * h_flat * reset_gate * (1.0 - reset_gate)], axis=-1).astype(jnp.bfloat16)
    grad_w_gate = jnp.dot(patch_gate.T, d_gate_pre, preferred_element_type=jnp.float32)
    grid_gate = unpatch(jnp.dot(d_gate_pre, w_gate.T, preferred_element_type=jnp.float32), tile_count, tile_side, 2 * channels)
    back_gate = settle(grid_gate, deliver(rim_of(grid_gate), target, flipped))
    grad_x = (back_cand[..., :channels] + back_gate[..., :channels]).astype(jnp.bfloat16)
    direct = (grad_flat * (1.0 - update_gate) + d_rh * reset_gate).reshape(tile_count, tile_side, tile_side, channels)
    grad_h = (direct + back_gate[..., channels:]).astype(jnp.bfloat16)
    return grad_x, grad_h, grad_w_gate, grad_w_cand
```

```python
import jax
import jax.numpy as jnp
from jax import lax
from jax.sharding import PartitionSpec as P


def both_neighbours(strips):
    size = lax.axis_size("tile")
    up = [(i, (i + 1) % size) for i in range(size)]
    down = [(j, i) for i, j in up]
    before = lax.ppermute(strips, "tile", up)
    after = lax.ppermute(strips, "tile", down)
    return before, after


def delivered(strips, chooser):
    before, after = both_neighbours(strips)
    flat = jnp.concatenate([before, after], axis=0).reshape(chooser.shape[1], -1)
    picked = jnp.dot(chooser, flat, preferred_element_type=jnp.float32)
    return picked.reshape(strips.shape)


def edge_strips(single):
    return jnp.stack([single[0], single[:, -1], single[-1], single[:, 0]], axis=0)


def framed(single, arrived):
    middle = jnp.concatenate([arrived[3][:, None], single, arrived[1][:, None]], axis=1)
    top = jnp.pad(arrived[0], ((1, 1), (0, 0)))
    bottom = jnp.pad(arrived[2], ((1, 1), (0, 0)))
    return jnp.concatenate([top[None], middle, bottom[None]], axis=0)


def patches_of(padded):
    tile_side = padded.shape[0] - 2
    columns = [
        padded[row_tap : row_tap + tile_side, col_tap : col_tap + tile_side]
        for row_tap in range(3)
        for col_tap in range(3)
    ]
    return jnp.concatenate(columns, axis=-1).reshape(tile_side * tile_side, 9 * padded.shape[-1])


def back_patches(grad):
    tile_side = grad.shape[0]
    wide = jnp.pad(grad, ((2, 2), (1, 1), (0, 0)))
    columns = [
        wide[2 - row_tap : 2 - row_tap + tile_side + 2, 2 - col_tap : 2 - col_tap + tile_side]
        for row_tap in range(3)
        for col_tap in range(3)
    ]
    return jnp.concatenate(columns, axis=-1).reshape((tile_side + 2) * tile_side, -1)


def side_patches(grad, col):
    tile_side = grad.shape[0]
    line = jnp.pad(grad[:, col], ((1, 1), (0, 0)))
    return jnp.concatenate([line[2 - t : 2 - t + tile_side] for t in range(3)], axis=-1)


def adjoint(grad, turned):
    tile_side, depth, width = grad.shape[0], turned.shape[2], turned.shape[3]
    grid = jnp.dot(
        back_patches(grad),
        turned.reshape(9 * depth, width),
        preferred_element_type=jnp.float32,
    ).reshape(tile_side + 2, tile_side, width)
    left = jnp.dot(
        side_patches(grad, 0),
        turned[:, 0].reshape(3 * depth, width),
        preferred_element_type=jnp.float32,
    )
    right = jnp.dot(
        side_patches(grad, tile_side - 1),
        turned[:, 2].reshape(3 * depth, width),
        preferred_element_type=jnp.float32,
    )
    return grid[1:-1], jnp.stack([grid[0], right, grid[-1], left], axis=0)


def settle(interior, arrived):
    last = interior.shape[0] - 1
    row_zero, row_last = ((0, last), (0, 0), (0, 0)), ((last, 0), (0, 0), (0, 0))
    col_zero, col_last = ((0, 0), (0, last), (0, 0)), ((0, 0), (last, 0), (0, 0))
    return (
        interior
        + jnp.pad(arrived[0][None], row_zero)
        + jnp.pad(arrived[2][None], row_last)
        + jnp.pad(arrived[3][:, None], col_zero)
        + jnp.pad(arrived[1][:, None], col_last)
    )


def contract(patch_rows, grad_rows):
    return jnp.einsum(
        "ck,co->ko", patch_rows, grad_rows, preferred_element_type=jnp.float32
    ).astype(jnp.bfloat16)


def scatter_sum(part):
    size = lax.axis_size("tile")
    place = lax.axis_index("tile")
    rows = part.shape[0] // size
    blocks = part.reshape(size, rows, part.shape[1])
    step = 1
    while step < size:
        pairs = blocks.reshape(blocks.shape[0] // 2, 2, rows, part.shape[1])
        mine = (place // step) % 2
        keep = lax.dynamic_index_in_dim(pairs, mine, 1, keepdims=False)
        send = lax.dynamic_index_in_dim(pairs, 1 - mine, 1, keepdims=False)
        got = lax.ppermute(send, "tile", [(i, i ^ step) for i in range(size)])
        blocks = keep.astype(jnp.float32) + got.astype(jnp.float32)
        step *= 2
        if step < size:
            blocks = blocks.astype(jnp.bfloat16)
    return blocks.reshape(rows, part.shape[1]).astype(jnp.float32)


def turned_kernel(weights, channels_out):
    return weights.reshape(3, 3, -1, channels_out).transpose(0, 1, 3, 2)


def routing_matrix(partner_edge, edge_flip, tile_slot, tile_side):
    tile_count = lax.axis_size("tile")
    my_slot = lax.axis_index("tile")
    slot_range = jnp.arange(tile_count, dtype=jnp.int32)
    is_mine = (tile_slot == my_slot)[:, None]
    partners = jnp.sum(jnp.where(is_mine, partner_edge, 0), axis=0)
    flip_bits = jnp.sum(jnp.where(is_mine, edge_flip, 0), axis=0)
    partner_slot = jnp.sum(
        jnp.where(slot_range[None, :] == (partners // 4)[:, None], tile_slot[None, :], 0), axis=1
    )
    from_next = (partner_slot - my_slot) % tile_count == 1
    line = jnp.where(from_next, 4, 0) + partners % 4
    cells = jnp.arange(tile_side, dtype=jnp.int32)
    cell = jnp.where(flip_bits[:, None] == 1, tile_side - 1 - cells[None, :], cells[None, :])
    source = (line[:, None] * tile_side + cell).reshape(-1)
    return (source[:, None] == jnp.arange(8 * tile_side, dtype=jnp.int32)[None, :]).astype(
        jnp.bfloat16
    )


def shards(
    x_tiles, h_tiles, grad_out, w_gate, b_gate, w_cand, b_cand, partner_edge, edge_flip, tile_slot
):
    tile_side = x_tiles.shape[1]
    channels = x_tiles.shape[3]
    cells = (tile_side, tile_side, channels)
    x_single = x_tiles[0]
    h_single = h_tiles[0]
    joined = jnp.concatenate([x_single, h_single], axis=-1)
    chooser = routing_matrix(partner_edge, edge_flip, tile_slot, tile_side)
    turned_cand = turned_kernel(w_cand, channels)
    turned_gate = turned_kernel(w_gate, 2 * channels)

    arrived = delivered(edge_strips(joined), chooser).astype(jnp.bfloat16)
    padded_gate = framed(joined, arrived)
    patch_gate = patches_of(padded_gate)
    gate_act = jax.nn.sigmoid(
        jnp.dot(patch_gate, w_gate, preferred_element_type=jnp.float32) + b_gate
    )
    update_gate = gate_act[:, :channels]
    reset_gate = gate_act[:, channels:]
    h_flat = h_single.reshape(-1, channels).astype(jnp.float32)
    reset_h = (reset_gate * h_flat).astype(jnp.bfloat16).reshape(cells)

    arrived_reset = delivered(edge_strips(reset_h), chooser).astype(jnp.bfloat16)
    padded_reset = framed(reset_h, arrived_reset)
    patch_cand = patches_of(jnp.concatenate([padded_gate[..., :channels], padded_reset], axis=-1))
    candidate = jnp.tanh(jnp.dot(patch_cand, w_cand, preferred_element_type=jnp.float32) + b_cand)
    grad_flat = grad_out[0].reshape(-1, channels).astype(jnp.float32)
    d_cand_pre = (grad_flat * update_gate * (1.0 - candidate * candidate)).astype(jnp.bfloat16)
    d_update_pre = (
        grad_flat * (candidate - h_flat) * update_gate * (1.0 - update_gate)
    ).astype(jnp.bfloat16)

    inner_cand, rim_cand = adjoint(d_cand_pre.reshape(cells), turned_cand)
    arrived_rh = delivered(rim_cand[..., channels:].astype(jnp.bfloat16), chooser)
    d_rh = settle(inner_cand[..., channels:], arrived_rh).reshape(-1, channels)

    grad_w_cand = scatter_sum(contract(patch_cand, d_cand_pre))
    grad_w_update = scatter_sum(contract(patch_gate, d_update_pre))

    d_reset_pre = (d_rh * h_flat * reset_gate * (1.0 - reset_gate)).astype(jnp.bfloat16)
    grad_w_reset = scatter_sum(contract(patch_gate, d_reset_pre))
    d_gate_pre = jnp.concatenate([d_update_pre, d_reset_pre], axis=-1)
    inner_gate, rim_gate = adjoint(
        d_gate_pre.reshape(tile_side, tile_side, 2 * channels), turned_gate
    )
    rim_x = rim_gate[..., :channels] + rim_cand[..., :channels]
    rims = jnp.concatenate([rim_x, rim_gate[..., channels:]], axis=-1).astype(jnp.bfloat16)
    arrived_gate = delivered(rims, chooser)
    grad_x = settle(
        inner_gate[..., :channels] + inner_cand[..., :channels], arrived_gate[..., :channels]
    ).astype(jnp.bfloat16)
    direct = (grad_flat * (1.0 - update_gate) + d_rh * reset_gate).reshape(cells)
    grad_h = settle(direct + inner_gate[..., channels:], arrived_gate[..., channels:]).astype(
        jnp.bfloat16
    )
    grad_w_gate = jnp.concatenate([grad_w_update, grad_w_reset], axis=-1)
    return (grad_x[None], grad_h[None], grad_w_gate, grad_w_cand)


def solution(mesh):
    in_specs = (
        P(("grp", "tile"), None, None, None),
        P(("grp", "tile"), None, None, None),
        P(("grp", "tile"), None, None, None),
        P(),
        P(),
        P(),
        P(),
        P(),
        P(),
        P(),
    )
    out_specs = (
        P(("grp", "tile"), None, None, None),
        P(("grp", "tile"), None, None, None),
        P(("grp", "tile"), None),
        P(("grp", "tile"), None),
    )
    return jax.shard_map(shards, mesh=mesh, in_specs=in_specs, out_specs=out_specs, check_vma=False)
```

```python
import jax
import jax.numpy as jnp
from jax import lax
from jax.sharding import PartitionSpec as P


def both_neighbours(strips):
    size = lax.axis_size("tile")
    up = [(i, (i + 1) % size) for i in range(size)]
    down = [(j, i) for i, j in up]
    before = lax.ppermute(strips, "tile", up)
    after = lax.ppermute(strips, "tile", down)
    return before, after


def delivered(strips, chooser):
    before, after = both_neighbours(strips)
    flat = jnp.concatenate([before, after], axis=0).reshape(chooser.shape[1], -1)
    picked = jnp.dot(chooser, flat, preferred_element_type=jnp.float32)
    return picked.reshape(strips.shape)


def edge_strips(single):
    return jnp.stack([single[0], single[:, -1], single[-1], single[:, 0]], axis=0)


def framed(single, arrived):
    middle = jnp.concatenate([arrived[3][:, None], single, arrived[1][:, None]], axis=1)
    top = jnp.pad(arrived[0], ((1, 1), (0, 0)))
    bottom = jnp.pad(arrived[2], ((1, 1), (0, 0)))
    return jnp.concatenate([top[None], middle, bottom[None]], axis=0)


def patches_of(padded):
    tile_side = padded.shape[0] - 2
    columns = [
        padded[row_tap : row_tap + tile_side, col_tap : col_tap + tile_side]
        for row_tap in range(3)
        for col_tap in range(3)
    ]
    return jnp.concatenate(columns, axis=-1).reshape(tile_side * tile_side, 9 * padded.shape[-1])


def back_patches(grad):
    tile_side = grad.shape[0]
    wide = jnp.pad(grad, ((2, 2), (1, 1), (0, 0)))
    blocks = [
        wide[2 - row_tap : 2 - row_tap + tile_side + 2, 2 - col_tap : 2 - col_tap + tile_side]
        for row_tap in range(3)
        for col_tap in range(3)
    ]
    return jnp.stack(blocks, axis=0).reshape(9, (tile_side + 2) * tile_side, -1)


def side_patches(grad, col):
    tile_side = grad.shape[0]
    line = jnp.pad(grad[:, col], ((1, 1), (0, 0)))
    return jnp.stack([line[2 - t : 2 - t + tile_side] for t in range(3)], axis=0)


def tap_dot(patches, taps):
    return lax.conv_general_dilated(
        patches,
        taps,
        window_strides=(1,),
        padding="VALID",
        dimension_numbers=("WNC", "WOI", "WNC"),
        preferred_element_type=jnp.float32,
    )[0]


def adjoint(grad, weights):
    tile_side, depth = grad.shape[0], grad.shape[2]
    taps = weights.reshape(3, 3, -1, depth)
    width = taps.shape[2]
    grid = tap_dot(back_patches(grad), taps.reshape(9, width, depth)).reshape(
        tile_side + 2, tile_side, width
    )
    left = tap_dot(side_patches(grad, 0), taps[:, 0])
    right = tap_dot(side_patches(grad, tile_side - 1), taps[:, 2])
    return grid[1:-1], jnp.stack([grid[0], right, grid[-1], left], axis=0)


def settle(interior, arrived):
    last = interior.shape[0] - 1
    row_zero, row_last = ((0, last), (0, 0), (0, 0)), ((last, 0), (0, 0), (0, 0))
    col_zero, col_last = ((0, 0), (0, last), (0, 0)), ((0, 0), (last, 0), (0, 0))
    return (
        interior
        + jnp.pad(arrived[0][None], row_zero)
        + jnp.pad(arrived[2][None], row_last)
        + jnp.pad(arrived[3][:, None], col_zero)
        + jnp.pad(arrived[1][:, None], col_last)
    )


def contract(patch_rows, grad_rows):
    return jnp.einsum(
        "ck,co->ko", patch_rows, grad_rows, preferred_element_type=jnp.float32
    ).astype(jnp.bfloat16)


def scatter_sum(part):
    size = lax.axis_size("tile")
    place = lax.axis_index("tile")
    rows = part.shape[0] // size
    blocks = part.reshape(size, rows, part.shape[1])
    step = 1
    while step < size:
        pairs = blocks.reshape(blocks.shape[0] // 2, 2, rows, part.shape[1])
        mine = (place // step) % 2
        keep = lax.dynamic_index_in_dim(pairs, mine, 1, keepdims=False)
        send = lax.dynamic_index_in_dim(pairs, 1 - mine, 1, keepdims=False)
        got = lax.ppermute(send.astype(jnp.bfloat16), "tile", [(i, i ^ step) for i in range(size)])
        blocks = keep.astype(jnp.float32) + got.astype(jnp.float32)
        step *= 2
    return blocks.reshape(rows, part.shape[1]).astype(jnp.float32)


def routing_matrix(partner_edge, edge_flip, tile_slot, tile_side):
    tile_count = lax.axis_size("tile")
    my_slot = lax.axis_index("tile")
    slot_range = jnp.arange(tile_count, dtype=jnp.int32)
    is_mine = (tile_slot == my_slot)[:, None]
    partners = jnp.sum(jnp.where(is_mine, partner_edge, 0), axis=0)
    flip_bits = jnp.sum(jnp.where(is_mine, edge_flip, 0), axis=0)
    partner_slot = jnp.sum(
        jnp.where(slot_range[None, :] == (partners // 4)[:, None], tile_slot[None, :], 0), axis=1
    )
    from_next = (partner_slot - my_slot) % tile_count == 1
    line = jnp.where(from_next, 4, 0) + partners % 4
    cells = jnp.arange(tile_side, dtype=jnp.int32)
    cell = jnp.where(flip_bits[:, None] == 1, tile_side - 1 - cells[None, :], cells[None, :])
    source = (line[:, None] * tile_side + cell).reshape(-1)
    return (source[:, None] == jnp.arange(8 * tile_side, dtype=jnp.int32)[None, :]).astype(
        jnp.bfloat16
    )


def cell_backward(
    x_tiles, h_tiles, grad_out, w_gate, b_gate, w_cand, b_cand, partner_edge, edge_flip, tile_slot
):
    tile_side = x_tiles.shape[1]
    channels = x_tiles.shape[3]
    cells = (tile_side, tile_side, channels)
    x_single = x_tiles[0]
    h_single = h_tiles[0]
    joined = jnp.concatenate([x_single, h_single], axis=-1)
    chooser = routing_matrix(partner_edge, edge_flip, tile_slot, tile_side)

    arrived = delivered(edge_strips(joined), chooser).astype(jnp.bfloat16)
    padded_gate = framed(joined, arrived)
    patch_gate = patches_of(padded_gate)
    gate_act = jax.nn.sigmoid(
        jnp.dot(patch_gate, w_gate, preferred_element_type=jnp.float32) + b_gate
    )
    update_gate = gate_act[:, :channels]
    reset_gate = gate_act[:, channels:]
    h_flat = h_single.reshape(-1, channels).astype(jnp.float32)
    reset_h = (reset_gate * h_flat).astype(jnp.bfloat16).reshape(cells)

    arrived_reset = delivered(edge_strips(reset_h), chooser).astype(jnp.bfloat16)
    padded_reset = framed(reset_h, arrived_reset)
    patch_cand = patches_of(jnp.concatenate([padded_gate[..., :channels], padded_reset], axis=-1))
    candidate = jnp.tanh(jnp.dot(patch_cand, w_cand, preferred_element_type=jnp.float32) + b_cand)
    grad_flat = grad_out[0].reshape(-1, channels).astype(jnp.float32)
    d_cand_pre = (grad_flat * update_gate * (1.0 - candidate * candidate)).astype(jnp.bfloat16)
    d_update_pre = (
        grad_flat * (candidate - h_flat) * update_gate * (1.0 - update_gate)
    ).astype(jnp.bfloat16)

    inner_cand, rim_cand = adjoint(d_cand_pre.reshape(cells), w_cand)
    arrived_rh = delivered(rim_cand[..., channels:].astype(jnp.bfloat16), chooser)
    d_rh = settle(inner_cand[..., channels:], arrived_rh).reshape(-1, channels)

    grad_w_cand = scatter_sum(contract(patch_cand, d_cand_pre))
    grad_w_update = scatter_sum(contract(patch_gate, d_update_pre))

    d_reset_pre = (d_rh * h_flat * reset_gate * (1.0 - reset_gate)).astype(jnp.bfloat16)
    grad_w_reset = scatter_sum(contract(patch_gate, d_reset_pre))
    d_gate_pre = jnp.concatenate([d_update_pre, d_reset_pre], axis=-1)
    inner_gate, rim_gate = adjoint(
        d_gate_pre.reshape(tile_side, tile_side, 2 * channels), w_gate
    )
    rim_x = rim_gate[..., :channels] + rim_cand[..., :channels]
    rims = jnp.concatenate([rim_x, rim_gate[..., channels:]], axis=-1).astype(jnp.bfloat16)
    arrived_gate = delivered(rims, chooser)
    grad_x = settle(
        inner_gate[..., :channels] + inner_cand[..., :channels], arrived_gate[..., :channels]
    ).astype(jnp.bfloat16)
    direct = (grad_flat * (1.0 - update_gate) + d_rh * reset_gate).reshape(cells)
    grad_h = settle(direct + inner_gate[..., channels:], arrived_gate[..., channels:]).astype(
        jnp.bfloat16
    )
    grad_w_gate = jnp.concatenate([grad_w_update, grad_w_reset], axis=-1)
    return (grad_x[None], grad_h[None], grad_w_gate, grad_w_cand)


def solution(mesh):
    in_specs = (
        P(("grp", "tile"), None, None, None),
        P(("grp", "tile"), None, None, None),
        P(("grp", "tile"), None, None, None),
        P(),
        P(),
        P(),
        P(),
        P(),
        P(),
        P(),
    )
    out_specs = (
        P(("grp", "tile"), None, None, None),
        P(("grp", "tile"), None, None, None),
        P(("grp", "tile"), None),
        P(("grp", "tile"), None),
    )
    return jax.shard_map(cell_backward, mesh=mesh, in_specs=in_specs, out_specs=out_specs, check_vma=False)
```
